32 devices in a mesh: row: 4 (over y, x), col: 8 (over z, core).
Axes of the slice: x: 2, y: 2, z: 4, core: 2. Of those that a mesh axis runs over, the one named last changes fastest.
Arguments:
- tokens: bfloat16 [256, 16384], P('row', 'col'), may hold values from -6 to 6
- grad_out: bfloat16 [256, 16384], P('row', 'col'), may hold values from -6 to 6
- w_gate: bfloat16 [16384, 26624], P('col', 'row'), may hold values from -0.046875 to 0.046875
- w_up: bfloat16 [16384, 26624], P('col', 'row'), may hold values from -0.046875 to 0.046875
- w_down: bfloat16 [26624, 16384], P('row', 'col'), may hold values from -0.0390625 to 0.0390625
- radius: float32 [1], replicated, may hold values from 8 to 24
Outputs:
- perturbed_out: bfloat16 [256, 16384], P('row', 'col')
- grad_norm: float32 [1], replicated
The draws below stay inside these ranges and needn't reach their ends.
All inputs are finite; a program needn't handle non-finite values.
Results may differ from the reference program's by a relative error of at most 0.02.
Values may be sent and summed in bfloat16 or wider, within the bound.
A program may use at most 384 MiB of HBM per device.

```python
import math
import jax
import jax.numpy as jnp
from jax import lax

D = 16384
FFW = 26624
TOK = 256


def strengthened(drawn, own_key, source, target, blocks, factor):
    owner, partner = [(jnp.arange(drawn.shape[dim]) // (drawn.shape[dim] // blocks)).reshape([-1 if axis == dim else 1 for axis in range(drawn.ndim)]) for dim in (source, target)]
    chosen = jax.random.permutation(own_key, blocks)[partner]
    strong = (owner == chosen) | (owner == (partner + blocks // 2) % blocks)
    return jnp.where(strong, factor * drawn, drawn)


def block_scale(rng, extent, split, smallest, largest):
    level = 1.0
    for axis_at, parts in split:
        draws = jax.random.uniform(jax.random.fold_in(jax.random.fold_in(rng, 6), axis_at), (parts,), jnp.float32, smallest / len(split), largest / len(split))
        level = level * jnp.repeat(jnp.exp(draws), extent[axis_at] // parts).reshape((-1,) + (1,) * (len(extent) - 1 - axis_at))
    return level


def noise(rng, extent, deviation, bound, pieces=(), kind=jnp.bfloat16):
    drawn = jax.random.normal(rng, extent, jnp.float32) * deviation
    if len(pieces) > 0:
        drawn = block_scale(rng, extent, pieces, -0.22, 0.18) * drawn
    return jnp.clip(drawn, min=-bound, max=bound).astype(kind)


def heavy_noise(own_key, shape, scale, reach, split, heavy, kind=jnp.bfloat16):
    values = scale * jax.random.normal(own_key, shape, jnp.float32)
    if split:
        values = values * block_scale(own_key, shape, split, -0.22, 0.18)
    return jnp.clip(strengthened(values, jax.random.fold_in(own_key, 3), *heavy), -reach, reach).astype(kind)


def setup_inputs(seed: int = 0) -> dict:
    keys = jax.random.split(jax.random.key(seed), 7)
    tokens = heavy_noise(keys[0], (TOK, D), 1.0, 6.0, ((0, 4), (1, 8)), (1, 0, 8, 2.0))
    grad_out = heavy_noise(keys[1], (TOK, D), 1.0, 6.0, ((0, 4), (1, 8)), (1, 0, 8, 2.0))
    w_gate = noise(keys[2], (D, FFW), D ** -0.5, 0.046875, ((0, 8), (1, 4)))
    w_up = noise(keys[3], (D, FFW), D ** -0.5, 0.046875, ((0, 8), (1, 4)))
    w_down = noise(keys[4], (FFW, D), FFW ** -0.5, 0.0390625, ((0, 4), (1, 8)))
    radius = jnp.clip(jax.random.uniform(keys[5], (1,), jnp.float32, 8.0, 24.0), 8.0, 24.0)
    return {"tokens": tokens, "grad_out": grad_out, "w_gate": w_gate, "w_up": w_up, "w_down": w_down, "radius": radius}


def tdot(left, right):
    return lax.dot_general(left, right, (((0,), (0,)), ((), ())), preferred_element_type=jnp.float32)

def block_grads(tokens, grad_out, w_gate, w_up, w_down, index, width):
    start = (index * width).astype(jnp.int32)
    gate_blk = lax.dynamic_slice_in_dim(w_gate, start, width, 1)
    up_blk = lax.dynamic_slice_in_dim(w_up, start, width, 1)
    down_blk = lax.dynamic_slice_in_dim(w_down, start, width, 0)
    gate = jnp.dot(tokens, gate_blk, preferred_element_type=jnp.float32)
    upval = jnp.dot(tokens, up_blk, preferred_element_type=jnp.float32)
    sig = jax.nn.sigmoid(gate)
    silu = gate * sig
    hidden = (silu * upval).astype(jnp.bfloat16)
    grad_down = tdot(hidden, grad_out)
    grad_hidden = lax.dot_general(grad_out, down_blk, (((1,), (1,)), ((), ())), preferred_element_type=jnp.float32).astype(jnp.bfloat16).astype(jnp.float32)
    grad_gate_act = (grad_hidden * upval * sig * (1.0 + gate * (1.0 - sig))).astype(jnp.bfloat16)
    grad_up_act = (grad_hidden * silu).astype(jnp.bfloat16)
    grad_gate = tdot(tokens, grad_gate_act)
    grad_up = tdot(tokens, grad_up_act)
    return (grad_gate, grad_up, grad_down, gate_blk, up_blk, down_blk)

def reference(tokens, grad_out, w_gate, w_up, w_down, radius):
    nblocks = math.gcd(FFW, 16)
    width = FFW // nblocks
    indices = jnp.arange(nblocks, dtype=jnp.int32)

    def first(carry, index):
        grad_gate, grad_up, grad_down, a_blk, b_blk, c_blk = block_grads(tokens, grad_out, w_gate, w_up, w_down, index, width)
        part = jnp.sum(grad_gate * grad_gate) + jnp.sum(grad_up * grad_up) + jnp.sum(grad_down * grad_down)
        return (carry + part, None)
    total, unused = lax.scan(first, jnp.zeros((), jnp.float32), indices)
    scale = radius[0] * lax.rsqrt(total + 1e-06)

    def second(carry, index):
        grad_gate, grad_up, grad_down, gate_blk, up_blk, down_blk = block_grads(tokens, grad_out, w_gate, w_up, w_down, index, width)
        gate_pert = (gate_blk.astype(jnp.float32) + scale * grad_gate).astype(jnp.bfloat16)
        up_pert = (up_blk.astype(jnp.float32) + scale * grad_up).astype(jnp.bfloat16)
        down_pert = (down_blk.astype(jnp.float32) + scale * grad_down).astype(jnp.bfloat16)
        pgate = jnp.dot(tokens, gate_pert, preferred_element_type=jnp.float32)
        pup = jnp.dot(tokens, up_pert, preferred_element_type=jnp.float32)
        phidden = (jax.nn.silu(pgate) * pup).astype(jnp.bfloat16)
        return (carry + jnp.dot(phidden, down_pert, preferred_element_type=jnp.float32), None)
    summed, unused = lax.scan(second, jnp.zeros((TOK, D), jnp.float32), indices)
    return (summed.astype(jnp.bfloat16), jnp.sqrt(total).reshape(1))
```

```python
import functools

import jax
import jax.numpy as jnp
from jax import lax
from jax.sharding import PartitionSpec as P

F32 = jnp.float32
BF16 = jnp.bfloat16


def contract(left, right, left_dim, right_dim):
    return lax.dot_general(
        left, right, (((left_dim,), (right_dim,)), ((), ())), preferred_element_type=F32
    )


class Grid:
    def __init__(self, cols, rows):
        self.cols, self.rows, self.chips = cols, rows, cols // 2
        self.at = lax.axis_index("col")
        self.chip, self.core = self.at // 2, self.at % 2
        self.sign = 1 - 2 * self.core
        self.swap = [(i, i ^ 1) for i in range(cols)]
        self.ring = [
            (2 * chip + core, 2 * ((chip + 1 - 2 * core) % self.chips) + core)
            for chip in range(self.chips)
            for core in range(2)
        ]

    def block(self, step):
        return (self.chip - self.sign * step) % self.chips

    def scatter(self, partial):
        blocks = partial.astype(BF16).reshape(2, -1, partial.shape[1])
        other = lax.dynamic_index_in_dim(blocks, 1 - self.core, 0, keepdims=False)
        other = lax.ppermute(other, "col", self.swap)
        rows = partial.shape[0] // self.cols

        def pair_sum(step):
            here = self.block(step)
            mine = lax.dynamic_slice_in_dim(
                blocks.reshape(partial.shape), (self.core * self.chips + here) * rows, rows, 0
            )
            theirs = lax.dynamic_slice_in_dim(other, here * rows, rows, 0)
            return mine.astype(F32) + theirs.astype(F32)

        return pair_sum

    def travel(self, pair_sum, running):
        for step in range(2, self.chips + 1):
            running = lax.ppermute(running.astype(BF16), "col", self.ring).astype(F32) + pair_sum(step)
        return running

    def gather(self, own):
        result = jnp.zeros((2, self.chips) + own.shape, own.dtype)
        held = own
        for step in range(self.chips):
            other = lax.ppermute(held, "col", self.swap)
            result = lax.dynamic_update_slice(result, held[None, None], (self.core, self.block(step), 0, 0))
            from_other = (self.chip + self.sign * step) % self.chips
            result = lax.dynamic_update_slice(result, other[None, None], (1 - self.core, from_other, 0, 0))
            if step < self.chips - 1:
                held = lax.ppermute(held, "col", self.ring)
        return result.reshape(-1, own.shape[1])

    def total(self, value, axis, size, kind):
        bit = 1
        while bit < size:
            moved = lax.ppermute(value.astype(kind), axis, [(i, i ^ bit) for i in range(size)])
            value = value.astype(kind).astype(F32) + moved.astype(F32)
            bit *= 2
        return value

    def row_shift(self, value, flip):
        return lax.ppermute(value, "row", [(i, i ^ flip) for i in range(self.rows)])

    def row_gather(self, own):
        at = lax.axis_index("row")
        result = jnp.zeros((self.rows,) + own.shape, own.dtype)
        for flip in range(self.rows):
            block = own if flip == 0 else self.row_shift(own, flip)
            result = lax.dynamic_update_slice(result, block[None], (at ^ flip, 0, 0))
        return result.reshape(-1, own.shape[1])

    def row_scatter(self, partial):
        at = lax.axis_index("row")
        blocks = partial.reshape(self.rows, -1, partial.shape[1])
        total = lax.dynamic_index_in_dim(blocks, at, 0, keepdims=False).astype(F32)
        for flip in range(1, self.rows):
            sent = lax.dynamic_index_in_dim(blocks, at ^ flip, 0, keepdims=False)
            total = total + self.row_shift(sent.astype(BF16), flip).astype(F32)
        return total


def per_device(grid_shape, tokens, grad_out, w_gate, w_up, w_down, radius):
    grid = Grid(*grid_shape)
    x = grid.row_gather(tokens)
    dy = grid.row_gather(grad_out)
    grams = jnp.concatenate([contract(x, x, 1, 1), contract(dy, dy, 1, 1)], 0)
    x_first, grams = lax.optimization_barrier((x, grams))
    grams = lax.psum(grams, "col")

    gate_partial = contract(w_gate, x_first, 0, 1).astype(BF16)
    gate_partial, x_next = lax.optimization_barrier((gate_partial, x_first))
    gate_sum = grid.scatter(gate_partial)
    up_partial = contract(w_up, x_next, 0, 1).astype(BF16)
    gate_sent = gate_sum(1).astype(BF16)
    up_partial, gate_sent, dy_next = lax.optimization_barrier((up_partial, gate_sent, dy))
    up_sum = grid.scatter(up_partial)
    grad_hidden_sum = grid.scatter(contract(w_down, dy_next, 1, 1))
    gate = grid.travel(gate_sum, gate_sent)
    upval = grid.travel(up_sum, up_sum(1))
    grad_hidden = grid.travel(grad_hidden_sum, grad_hidden_sum(1)).astype(BF16).astype(F32)
    ntok = x.shape[0]
    gram_x, gram_dy = grams[:ntok], grams[ntok:]

    sig = jax.nn.sigmoid(gate)
    silu = gate * sig
    hidden = (silu * upval).astype(BF16)
    grad_gate_act = (grad_hidden * upval * sig * (1.0 + gate * (1.0 - sig))).astype(BF16)
    grad_up_act = (grad_hidden * silu).astype(BF16)

    act_gram = contract(grad_gate_act, grad_gate_act, 0, 0) + contract(grad_up_act, grad_up_act, 0, 0)
    local_squares = jnp.sum(gram_x * act_gram) + jnp.sum(gram_dy * contract(hidden, hidden, 0, 0))
    summed = jnp.full((8, 128), local_squares)
    for axis, size in (("col", grid.cols), ("row", grid.rows)):
        summed = grid.total(summed, axis, size, F32)
    total = jnp.maximum(summed[0, 0], 0.0)
    scale = radius[0] * lax.rsqrt(total + 1e-06)

    high = gram_x.astype(BF16)
    low = (gram_x - high.astype(F32)).astype(BF16)

    def step(act):
        return scale * (contract(act, high, 1, 0) + contract(act, low, 1, 0))

    phidden = (jax.nn.silu(gate + step(grad_gate_act)) * (upval + step(grad_up_act))).astype(BF16)
    mixing = grid.total(scale * contract(phidden, hidden, 0, 0), "col", grid.cols, BF16)
    phidden_all = grid.gather(phidden)
    partial_out = contract(phidden_all, w_down, 0, 0) + contract(
        mixing.astype(BF16), dy, 1, 0
    )
    perturbed_out = grid.row_scatter(partial_out.astype(BF16)).astype(BF16)
    return (perturbed_out, jnp.sqrt(total).reshape(1))


def solution(mesh):
    in_specs = (
        P("row", "col"),
        P("row", "col"),
        P("col", "row"),
        P("col", "row"),
        P("row", "col"),
        P(),
    )
    out_specs = (P("row", "col"), P())
    return jax.shard_map(
        functools.partial(per_device, (mesh.shape["col"], mesh.shape["row"])),
        mesh=mesh,
        in_specs=in_specs,
        out_specs=out_specs,
        check_vma=False,
    )
```
